32 devices in a mesh: ep: 16 (over z, y, x), rep: 2 (over core).
Axes of the slice: x: 2, y: 2, z: 4, core: 2. Of those that a mesh axis runs over, the one named last changes fastest.
Arguments:
- tokens: bfloat16 [4096, 1024], P(('ep', 'rep')), may hold values from -6 to 6
- expert_ids: int32 [4096, 6], P(('ep', 'rep')), may hold values from 0 to 15, all different within a row; in each aligned block of 128 rows (0 to 127, 128 to 255, ...) at most 49 rows name the same one
- gate_weights: float32 [4096, 6], P(('ep', 'rep')), may hold values from 0.1 to 0.5
- cotangent: bfloat16 [4096, 1024], P(('ep', 'rep')), may hold values from -6 to 6
- w_gate: bfloat16 [16, 1024, 704], P('ep', 'rep'), may hold values from -0.1875 to 0.1875
- w_up: bfloat16 [16, 1024, 704], P('ep', 'rep'), may hold values from -0.1875 to 0.1875
- w_down: bfloat16 [16, 704, 1024], P('ep', None, 'rep'), may hold values from -0.21875 to 0.21875
Outputs:
- mixed_out: bfloat16 [4096, 1024], P(('ep', 'rep'))
- grad_up: float32 [16, 1024, 704], P('ep', 'rep')
- grad_down: float32 [16, 704, 1024], P('ep', None, 'rep')
The draws below stay inside these ranges and needn't reach their ends.
Inputs may be any that keep to these rules, and one draw needn't show every extreme that they name: `expert_ids`: each token names 6 different experts. Of the tokens of one device, at most 49 name any one expert, and in every draw some expert is named by exactly 49 of some device's tokens.
All inputs are finite; a program needn't handle non-finite values.
Results may differ from the reference program's by a relative error of at most 0.012.
Values may be sent and summed in bfloat16 or wider, within the bound.
A program may use at most 128 MiB of HBM per device.

```python
import math
import jax
import jax.numpy as jnp
import numpy as np
from jax import lax

D = 1024
H = 704
TOP = 6
TOK_DEV = 128
EXPERTS = 16
CAP = 49
TOKENS = 4096
N_EP = 16
N_REP = 2


def block_scale(own_key, shape, split, low, high):
    factor_of, own = 1.0, jax.random.fold_in(own_key, 6)
    for dim, shards_of in split:
        heights = jnp.exp(jax.random.uniform(jax.random.fold_in(own, dim), (shards_of,), jnp.float32, low / len(split), high / len(split)))
        factor_of = factor_of * jnp.repeat(heights, shape[dim] // shards_of).reshape([-1 if axis == dim else 1 for axis in range(len(shape))])
    return factor_of


def routed_block(rng, own, number, rows, count, top, bound, slope):
    sequence = jax.random.permutation(rng, count)
    heavy_load, usual = portions_of(count, rows * top, bound, slope, True), portions_of(count, rows * top, bound, slope, False)
    places = jnp.arange(count)

    def named(sizes, rotation):
        used = int((sizes > 0).sum())
        fixed = max(1, used // 4)
        passed = fixed + (places - fixed + rotation * (used - fixed)) % max(1, count - fixed)
        return jnp.zeros((count,), jnp.int32).at[sequence[jnp.where(places < fixed, places, passed)]].set(jnp.asarray(sizes, jnp.int32))

    sizes = jnp.where(number % 4 == 0, named(heavy_load, number // 4), named(usual, number - number // 4 - 1))
    mixed = jax.random.permutation(jax.random.fold_in(own, 3), count)
    donor, sink = mixed[0:count // 2 * 2:2], mixed[1:count // 2 * 2:2]
    room = jnp.minimum(sizes[donor] - 1, bound - sizes[sink]) // 2
    room = jnp.where((donor == sequence[0]) | (sink == sequence[0]) | (sizes[sink] == 0), 0, jnp.maximum(room, 0))
    passed = jax.random.randint(jax.random.fold_in(own, 4), (count // 2,), 0, 1 << 20) % (room + 1)
    sizes = sizes.at[donor].add(-passed).at[sink].add(passed)
    members = jnp.searchsorted(jnp.cumsum(sizes), jnp.arange(rows * top), side="right").astype(jnp.int32)
    table = members.reshape(top, rows).T
    table = table[jax.random.permutation(jax.random.fold_in(own, 1), rows)]
    rotation = jax.random.randint(jax.random.fold_in(own, 2), (rows, 1), 0, top)
    return jnp.take_along_axis(table, (jnp.arange(top)[None, :] + rotation) % top, axis=1)


def portions_of(count, total, most, lean, full):
    loads = [(1 << 20) // math.isqrt(rank ** lean) + 1 for rank in range(1, count + 1)]
    largest = most if full else min(most, max(-(-total // count), total * loads[0] // sum(loads)))
    least = 1 if total - largest >= count - 1 else 0
    holding, spare = [largest] + [least] * (count - 1), total - largest - least * (count - 1)
    while spare > 0:
        movable = [i for i in range(1, count) if holding[i] < largest] or [i for i in range(1, count) if holding[i] < most]
        whole, left = sum([loads[i] for i in movable]), spare
        for i in movable:
            extra = min(most - holding[i], max(1, left * loads[i] // whole), spare)
            holding[i] = holding[i] + extra
            spare = spare - extra
    return np.array(holding)


def bell_draw(rng, dims, spread, most, split=(), kind=jnp.bfloat16):
    level = block_scale(rng, dims, split, -0.22, 0.18) if split else 1.0
    drawn = jax.random.normal(rng, dims, jnp.float32) * spread * level
    return jnp.minimum(jnp.maximum(drawn, -most), most).astype(kind)


def setup_inputs(seed: int = 0) -> dict:
    key_list = jax.random.split(jax.random.key(seed), 8)
    tokens = bell_draw(key_list[0], (TOKENS, D), 1.0, 6.0, ((0, 32),))
    expert_ids_keys = jax.random.split(jax.random.fold_in(key_list[1], 1), TOKENS // TOK_DEV)
    expert_ids_turns = jax.random.permutation(jax.random.fold_in(key_list[1], 3), TOKENS // TOK_DEV)
    expert_ids = jax.vmap(lambda own, number: routed_block(jax.random.fold_in(key_list[1], 2), own, number, TOK_DEV, EXPERTS, TOP, CAP, 2))(expert_ids_keys, expert_ids_turns).reshape((TOKENS, TOP))
    gate_weights = jnp.clip(0.1 + 0.4 * jax.random.uniform(key_list[2], (TOKENS, TOP), jnp.float32) ** block_scale(key_list[2], (TOKENS, TOP), ((0, 32),), -0.2, 0.2), 0.1, 0.5)
    cotangent = bell_draw(key_list[3], (TOKENS, D), 1.0, 6.0, ((0, 32),))
    w_gate = bell_draw(key_list[4], (EXPERTS, D, H), D ** -0.5, 0.1875, ((0, 16), (1, 2)))
    w_up = bell_draw(key_list[5], (EXPERTS, D, H), D ** -0.5, 0.1875, ((0, 16), (1, 2)))
    w_down = bell_draw(key_list[6], (EXPERTS, H, D), H ** -0.5, 0.21875, ((0, 16), (2, 2)))
    return {"tokens": tokens, "expert_ids": expert_ids, "gate_weights": gate_weights, "cotangent": cotangent, "w_gate": w_gate, "w_up": w_up, "w_down": w_down}


def reference(tokens, expert_ids, gate_weights, cotangent, w_gate, w_up, w_down):
    devices = N_EP * N_REP
    pair_count = TOK_DEV * TOP
    flat_ids = expert_ids.reshape(devices, pair_count).astype(jnp.int32)
    one_hot = (flat_ids[:, :, None] == jnp.arange(EXPERTS, dtype=jnp.int32)[None, None, :]).astype(jnp.int32)
    position = jnp.sum(one_hot * jnp.cumsum(one_hot, axis=1), axis=2) - 1
    device = jnp.arange(devices, dtype=jnp.int32)[:, None]
    source = device // N_REP
    rep_group = device % N_REP
    slot_index = (((flat_ids * N_REP + rep_group) * N_EP + source) * CAP + position).reshape(-1)
    slot_total = EXPERTS * N_REP * N_EP * CAP
    pair_index = jnp.arange(devices * pair_count, dtype=jnp.int32)
    owner_pair = jnp.zeros((slot_total,), jnp.int32).at[slot_index].set(pair_index)
    filled = jnp.zeros((slot_total,), jnp.float32).at[slot_index].set(1.0)
    owner_pair = owner_pair.reshape(EXPERTS, N_REP * N_EP * CAP)
    filled = filled.reshape(EXPERTS, N_REP * N_EP * CAP)
    gate_flat = gate_weights.reshape(-1).astype(jnp.float32)

    def expert_step(running, inputs):
        expert_owner, expert_filled, gate_shard, up_shard, down_shard = inputs
        token_rows = expert_owner // TOP
        arrived = tokens[token_rows] * expert_filled[:, None].astype(jnp.bfloat16)
        pair_scale = gate_flat[expert_owner] * expert_filled
        grad_rows = (pair_scale[:, None] * cotangent[token_rows].astype(jnp.float32)).astype(jnp.bfloat16)
        gate_pre = jnp.dot(arrived, gate_shard, preferred_element_type=jnp.float32)
        up_pre = jnp.dot(arrived, up_shard, preferred_element_type=jnp.float32)
        hidden = (jax.nn.silu(gate_pre) * up_pre).astype(jnp.bfloat16)
        expert_out = jnp.dot(hidden, down_shard, preferred_element_type=jnp.float32).astype(jnp.bfloat16)
        running = running.at[token_rows].add(pair_scale[:, None] * expert_out.astype(jnp.float32))
        hidden_grad = lax.dot_general(grad_rows, down_shard, (((1,), (1,)), ((), ())), preferred_element_type=jnp.float32)
        up_grad = (hidden_grad * jax.nn.silu(gate_pre)).astype(jnp.bfloat16)
        rows_group = arrived.reshape(N_REP, N_EP * CAP, D).astype(jnp.float32)
        up_group = up_grad.reshape(N_REP, N_EP * CAP, H).astype(jnp.float32)
        hidden_group = hidden.reshape(N_REP, N_EP * CAP, H).astype(jnp.float32)
        grad_group = grad_rows.reshape(N_REP, N_EP * CAP, D).astype(jnp.float32)
        part_up = jnp.einsum("grd,grh->gdh", rows_group, up_group, precision=lax.Precision.HIGHEST)
        part_down = jnp.einsum("grh,grd->ghd", hidden_group, grad_group, precision=lax.Precision.HIGHEST)
        part_up = lax.optimization_barrier(part_up.astype(jnp.bfloat16)).astype(jnp.float32)
        part_down = lax.optimization_barrier(part_down.astype(jnp.bfloat16)).astype(jnp.float32)
        return running, (jnp.sum(part_up, axis=0), jnp.sum(part_down, axis=0))

    start_sum = jnp.zeros((TOKENS, D), jnp.float32)
    mixed_sum, grads = lax.scan(expert_step, start_sum, (owner_pair, filled, w_gate, w_up, w_down))
    return mixed_sum.astype(jnp.bfloat16), grads[0], grads[1]
```

```python
import functools

import jax
import jax.numpy as jnp
from jax import lax
from jax.experimental import pallas as pl
from jax.experimental.pallas import tpu as pltpu
from jax.sharding import PartitionSpec as P

MESH = pl.DeviceIdType.MESH
F32 = jnp.float32
BF16 = jnp.bfloat16


def rows_of(count, unit):
    return -(-count // unit) * unit


def outer_of(ep_count):
    outer = 1
    while outer * outer < ep_count and ep_count % (outer * 2) == 0:
        outer *= 2
    return outer


def contract_rows(lhs, rhs):
    return lax.dot_general(lhs, rhs, (((0,), (0,)), ((), ())), preferred_element_type=F32)


def kernel(
    dims,
    meta_ref, tok_ref, cot_ref, wg_ref, wu_ref, wd_ref,
    mixed_ref, gup_ref, gdn_ref,
    metab, tokb, cotb, wgb, wub, wdb,
    slotb, gateb, pick, scale, mixhi, mixlo,
    sendx, recvx, sendg, recvg, sendo, recvo,
    gacc, uacc, hid, upg,
    comb, macc, sendz, recvz, supb, rupb, sdnb, rdnb,
    lsem, zs, zr, ps, pr, ys, yr, ws, wr, gs, gr,
):
    A, B, R, C, T, K, KP, cap, S, D, DC, H = dims
    CR = C // R
    ep = lax.axis_index("ep")
    rep = lax.axis_index("rep")
    oa, ob = ep // B, ep % B

    def out_peer(j):
        return {"ep": lax.rem(oa + j, A) * B + ob}

    def in_peer(j):
        return {"ep": oa * B + lax.rem(ob + j + B, B)}

    def rep_peer(j):
        return {"rep": lax.rem(rep + j, R)}

    peers = (
        [out_peer(j) for j in range(1, A)]
        + [in_peer(j) for j in range(1, B)]
        + [rep_peer(j) for j in range(1, R)]
    )

    def remote(src, dst, ssem, rsem, peer):
        copy = pltpu.make_async_remote_copy(
            src_ref=src, dst_ref=dst, send_sem=ssem, recv_sem=rsem,
            device_id=peer, device_id_type=MESH,
        )
        copy.start()
        return copy

    started = []
    local = {}

    def keep(src, dst, index):
        copy = pltpu.make_async_copy(src, dst, lsem.at[index])
        copy.start()
        return copy

    def cols(c):
        return pl.ds(c * DC, DC)

    for c in range(C):
        local["t", c] = keep(tok_ref.at[:, cols(c)], tokb.at[c, oa], c)
    local["g"] = keep(wg_ref, wgb.at[rep], 2 * C)
    local["u"] = keep(wu_ref, wub.at[rep], 2 * C + 1)
    local["d"] = keep(wd_ref, wdb.at[rep], 2 * C + 2)
    for c in range(C):
        local["c", c] = keep(cot_ref.at[:, cols(c)], cotb.at[c, oa], C + c)

    barrier = pltpu.get_barrier_semaphore()
    for peer in peers:
        pl.semaphore_signal(barrier, inc=1, device_id=peer, device_id_type=MESH)
    pl.semaphore_wait(barrier, len(peers))

    zc = {}
    for j in range(1, A):
        zc["m", j] = remote(meta_ref, metab.at[oa], zs.at[2 * C, j], zr.at[2 * C, j], out_peer(j))
    for c in range(C):
        for j in range(1, A):
            zc["t", c, j] = remote(
                tok_ref.at[:, cols(c)], tokb.at[c, oa], zs.at[c, j], zr.at[c, j], out_peer(j)
            )
    wc = {}
    for n, (src, dst) in enumerate(((wg_ref, wgb), (wu_ref, wub), (wd_ref, wdb))):
        for j in range(1, R):
            wc[n, j] = remote(src, dst.at[rep], ws.at[n, j], wr.at[n, j], rep_peer(j))
    for c in range(C):
        for j in range(1, A):
            zc["c", c, j] = remote(
                cot_ref.at[:, cols(c)], cotb.at[c, oa], zs.at[C + c, j], zr.at[C + c, j], out_peer(j)
            )
    started += list(zc.values()) + list(wc.values())

    metab[oa] = meta_ref[...]
    BP = slotb.shape[0]
    row = lax.broadcasted_iota(jnp.int32, (BP, T), 0)
    named = jnp.where(row < B, oa * B + lax.rem(ob + row, B), -1).astype(F32)
    earlier = (
        lax.broadcasted_iota(jnp.int32, (T, T), 0) < lax.broadcasted_iota(jnp.int32, (T, T), 1)
    ).astype(F32).astype(BF16)
    for j in range(1, A):
        zc["m", j].wait_recv()
    for a in range(A):
        member = jnp.zeros((BP, T), F32)
        weight = jnp.zeros((BP, T), F32)
        for k in range(K):
            same = metab[a, k : k + 1, :] == named
            member = member + jnp.where(same, 1.0, 0.0)
            weight = weight + jnp.where(same, metab[a, KP + k : KP + k + 1, :], 0.0)
        place = jnp.dot(member.astype(BF16), earlier, preferred_element_type=F32)
        slotb[:, a * T : (a + 1) * T] = jnp.where(member > 0.5, place + float(a * cap), -1.0)
        gateb[:, a * T : (a + 1) * T] = weight
    slot_id = lax.broadcasted_iota(jnp.int32, (S, A * T), 0).astype(F32)
    for b in range(B):
        hit = slotb[b : b + 1, :] == slot_id
        pick[b] = jnp.where(hit, 1.0, 0.0).astype(BF16)
        mix = jnp.where(hit, gateb[b : b + 1, :], 0.0)
        scale[b] = jnp.sum(mix, axis=1, keepdims=True)
        high = mix.astype(BF16)
        mixhi[b] = high
        mixlo[b] = (mix - high.astype(F32)).astype(BF16)

    pc = {}

    def pack_rows(c):
        local["t", c].wait()
        for j in range(1, A):
            zc["t", c, j].wait_recv()
        source = tokb[c].reshape(A * T, DC)
        for j in list(range(1, B)) + [0]:
            block = jnp.dot(pick[j], source, preferred_element_type=F32).astype(BF16)
            if j == 0:
                recvx[c, 0] = block
            else:
                sendx[c, j] = block
                pc["x", c, j] = remote(
                    sendx.at[c, j], recvx.at[c, j], ps.at[c, j], pr.at[c, j], in_peer(j)
                )

    def pack_grads(c):
        local["c", c].wait()
        for j in range(1, A):
            zc["c", c, j].wait_recv()
        source = cotb[c].reshape(A * T, DC)
        for j in list(range(1, B)) + [0]:
            block = jnp.dot(pick[j], source, preferred_element_type=F32)
            block = (block * scale[j]).astype(BF16)
            if j == 0:
                recvg[c, 0] = block
            else:
                sendg[c, j] = block
                pc["g", c, j] = remote(
                    sendg.at[c, j], recvg.at[c, j], ps.at[C + c, j], pr.at[C + c, j], in_peer(j)
                )

    for c in range(C):
        pack_rows(c)

    local["g"].wait()
    local["u"].wait()
    for j in range(1, R):
        wc[0, j].wait_recv()
        wc[1, j].wait_recv()
    for c in range(C):
        part = pl.ds((c % CR) * DC, DC)
        for j in range(1, B):
            pc["x", c, j].wait_recv()

        def gate_up(b, _, c=c, part=part):
            rows = recvx[c, b]
            gate = jnp.dot(rows, wgb[c // CR, part, :], preferred_element_type=F32)
            up = jnp.dot(rows, wub[c // CR, part, :], preferred_element_type=F32)
            if c > 0:
                gate = gate + gacc[b]
                up = up + uacc[b]
            if c < C - 1:
                gacc[b] = gate
                uacc[b] = up
            else:
                silu = gate / (1.0 + jnp.exp(-gate))
                gacc[b] = silu
                hid[b] = (silu * up).astype(BF16)
            return 0

        lax.fori_loop(0, B, gate_up, 0)
        pack_grads(c)

    local["d"].wait()
    for j in range(1, R):
        wc[2, j].wait_recv()
    for c in range(C):
        part = pl.ds((c % CR) * DC, DC)
        for j in list(range(1, B)) + [0]:
            block = jnp.dot(
                hid[j], wdb[c // CR, :, part], preferred_element_type=F32
            ).astype(BF16)
            if j == 0:
                recvo[c, 0] = block
            else:
                sendo[c, j] = block
                pc["o", c, j] = remote(
                    sendo.at[c, j], recvo.at[c, j],
                    ps.at[2 * C + c, j], pr.at[2 * C + c, j], in_peer(-j),
                )

    for c in range(C):
        part = pl.ds((c % CR) * DC, DC)
        for j in range(1, B):
            pc["g", c, j].wait_recv()

        def back(b, _, c=c, part=part):
            value = lax.dot_general(
                recvg[c, b], wdb[c // CR, :, part], (((1,), (1,)), ((), ())),
                preferred_element_type=F32,
            )
            if c > 0:
                value = value + uacc[b]
            if c < C - 1:
                uacc[b] = value
            else:
                upg[b] = (value * gacc[b]).astype(BF16)
            return 0

        lax.fori_loop(0, B, back, 0)

    hidden = lambda: hid[...].reshape(B * S, H)
    up_grad = lambda: upg[...].reshape(B * S, H)
    gc = {}
    for j in range(1, R):
        peer = lax.rem(rep + j, R)
        for i in range(CR):
            block = contract_rows(recvx[peer * CR + i].reshape(B * S, DC), up_grad())
            supb[j, i * DC : (i + 1) * DC, :] = block.astype(BF16)
        gc[0, j] = remote(supb.at[j], rupb.at[j], gs.at[0, j], gr.at[0, j], rep_peer(j))
        for i in range(CR):
            block = contract_rows(hidden(), recvg[peer * CR + i].reshape(B * S, DC))
            sdnb[j, :, i * DC : (i + 1) * DC] = block.astype(BF16)
        gc[1, j] = remote(sdnb.at[j], rdnb.at[j], gs.at[1, j], gr.at[1, j], rep_peer(j))

    yc = {}

    def combine(c):
        for j in range(1, B):
            pc["o", c, j].wait_recv()
        rows = recvo[c].reshape(B * S, DC)
        total = contract_rows(mixhi[...].reshape(B * S, A * T), rows)
        total = total + contract_rows(mixlo[...].reshape(B * S, A * T), rows)
        comb[...] = total.reshape(A, T, DC)
        sendz[c] = total.astype(BF16).reshape(A, T, DC)
        macc[c] = comb[oa]
        for j in range(1, A):
            yc[c, j] = remote(
                sendz.at[c, lax.rem(oa + j, A)], recvz.at[c, j],
                ys.at[c, j], yr.at[c, j], out_peer(j),
            )

    for c in range(C):
        combine(c)

    for i in range(CR):
        block = contract_rows(recvx[rep * CR + i].reshape(B * S, DC), up_grad())
        gup_ref[i * DC : (i + 1) * DC, :] = block.astype(BF16).astype(F32)
        block = contract_rows(hidden(), recvg[rep * CR + i].reshape(B * S, DC))
        gdn_ref[:, i * DC : (i + 1) * DC] = block.astype(BF16).astype(F32)
    for j in range(1, R):
        gc[0, j].wait_recv()
        gup_ref[...] += rupb[j].astype(F32)
        gc[1, j].wait_recv()
        gdn_ref[...] += rdnb[j].astype(F32)

    for c in range(C):
        total = macc[c]
        for j in range(1, A):
            yc[c, j].wait_recv()
            total = total + recvz[c, j].astype(F32)
        mixed_ref[:, c * DC : (c + 1) * DC] = total.astype(BF16)

    started += list(pc.values()) + list(gc.values()) + list(yc.values())
    for copy in started:
        copy.wait_send()


def local(tokens, expert_ids, gate_weights, cotangent, w_gate, w_up, w_down):
    ep_count, R = lax.axis_size("ep"), lax.axis_size("rep")
    T, D = tokens.shape
    K = expert_ids.shape[1]
    H = w_gate.shape[2]
    cap = T * K // ep_count + 1
    A = outer_of(ep_count)
    B = ep_count // A
    S = rows_of(A * cap, 16)
    DR = D // R
    DC = DR // 2 if DR % 256 == 0 else DR
    C = D // DC
    KP = rows_of(K, 8)
    BP = rows_of(B, 16)
    meta = jnp.concatenate(
        [
            jnp.pad(expert_ids.T.astype(F32), ((0, KP - K), (0, 0)), constant_values=-2.0),
            jnp.pad(gate_weights.T, ((0, KP - K), (0, 0))),
        ]
    )
    dims = (A, B, R, C, T, K, KP, cap, S, D, DC, H)
    vmem, dma = pltpu.VMEM, pltpu.SemaphoreType.DMA
    anywhere = pl.BlockSpec(memory_space=pl.ANY)
    inside = pl.BlockSpec(memory_space=pltpu.VMEM)
    blocks = vmem((C, B, S, DC), BF16)
    mixed, gup, gdn = pl.pallas_call(
        functools.partial(kernel, dims),
        out_shape=(
            jax.ShapeDtypeStruct((T, D), BF16),
            jax.ShapeDtypeStruct((DR, H), F32),
            jax.ShapeDtypeStruct((H, DR), F32),
        ),
        in_specs=[inside] + [anywhere] * 5,
        out_specs=[inside] * 3,
        scratch_shapes=[
            vmem((A, 2 * KP, T), F32),
            vmem((C, A, T, DC), BF16),
            vmem((C, A, T, DC), BF16),
            vmem((R, DR, H), BF16),
            vmem((R, DR, H), BF16),
            vmem((R, H, DR), BF16),
            vmem((BP, A * T), F32),
            vmem((BP, A * T), F32),
            vmem((B, S, A * T), BF16),
            vmem((B, S, 1), F32),
            vmem((B, S, A * T), BF16),
            vmem((B, S, A * T), BF16),
            blocks, blocks, blocks, blocks, blocks, blocks,
            vmem((B, S, H), F32),
            vmem((B, S, H), F32),
            vmem((B, S, H), BF16),
            vmem((B, S, H), BF16),
            vmem((A, T, DC), F32),
            vmem((C, T, DC), F32),
            vmem((C, A, T, DC), BF16),
            vmem((C, A, T, DC), BF16),
            vmem((R, DR, H), BF16),
            vmem((R, DR, H), BF16),
            vmem((R, H, DR), BF16),
            vmem((R, H, DR), BF16),
            dma((2 * C + 3,)),
            dma((2 * C + 1, A)), dma((2 * C + 1, A)),
            dma((3 * C, B)), dma((3 * C, B)),
            dma((C, A)), dma((C, A)),
            dma((3, R)), dma((3, R)),
            dma((2, R)), dma((2, R)),
        ],
        compiler_params=pltpu.CompilerParams(
            collective_id=0, has_side_effects=True, vmem_limit_bytes=62 * 1024 * 1024
        ),
    )(meta, tokens, cotangent, w_gate[0], w_up[0], w_down[0])
    return mixed, gup[None], gdn[None]


def solution(mesh):
    in_specs = (
        P(("ep", "rep"), None),
        P(("ep", "rep"), None),
        P(("ep", "rep"), None),
        P(("ep", "rep"), None),
        P("ep", "rep", None),
        P("ep", "rep", None),
        P("ep", None, "rep"),
    )
    out_specs = (P(("ep", "rep"), None), P("ep", "rep", None), P("ep", None, "rep"))
    return jax.shard_map(local, mesh=mesh, in_specs=in_specs, out_specs=out_specs, check_vma=False)
```

```python
import functools

import jax
import jax.numpy as jnp
from jax import lax
from jax.experimental import pallas as pl
from jax.experimental.pallas import tpu as pltpu
from jax.sharding import PartitionSpec as P

MESH = pl.DeviceIdType.MESH
F32 = jnp.float32
BF16 = jnp.bfloat16


def rows_of(count, unit):
    return -(-count // unit) * unit


def outer_of(ep_count):
    outer = 1
    while outer * outer < ep_count and ep_count % (outer * 2) == 0:
        outer *= 2
    return outer


def contract_columns(lhs, rhs):
    return lax.dot_general(lhs, rhs, (((1,), (1,)), ((), ())), preferred_element_type=F32)


def contract_rows(lhs, rhs):
    return lax.dot_general(lhs, rhs, (((0,), (0,)), ((), ())), preferred_element_type=F32)


def kernel(
    dims,
    meta_ref, tok_ref, cot_ref, wg_ref, wu_ref, wd_ref,
    mixed_ref, gup_ref, gdn_ref,
    metab, tokb, cotb, wgb, wub, wdb,
    slotb, gateb, pick, scale, mixhi, mixlo,
    sendx, recvx, sendg, recvg, sendo, recvo,
    gacc, uacc, hid, upg,
    comb, macc, sendz, recvz, supb, rupb, sdnb, rdnb,
    lsem, zs, zr, fs, ps, pr, ys, yr, ws, wr, gs, gr,
):
    A, B, R, C, T, K, KP, cap, S, D, DC, H, W = dims
    CR = C // R
    ep = lax.axis_index("ep")
    rep = lax.axis_index("rep")
    oa, ob = ep // B, ep % B

    def out_peer(j):
        return {"ep": lax.rem(oa + j, A) * B + ob}

    def in_peer(j):
        return {"ep": oa * B + lax.rem(ob + j + B, B)}

    def rep_peer(j):
        return {"rep": lax.rem(rep + j, R)}

    peers = (
        [out_peer(j) for j in range(1, A)]
        + [in_peer(j) for j in range(1, B)]
        + [rep_peer(j) for j in range(1, R)]
    )

    def build(src, dst, ssem, rsem, peer):
        return pltpu.make_async_remote_copy(
            src_ref=src, dst_ref=dst, send_sem=ssem, recv_sem=rsem,
            device_id=peer, device_id_type=MESH,
        )

    def remote(src, dst, ssem, rsem, peer):
        copy = build(src, dst, ssem, rsem, peer)
        copy.start()
        return copy

    started = []
    local = {}

    def keep(src, dst, index):
        copy = pltpu.make_async_copy(src, dst, lsem.at[index])
        copy.start()
        return copy

    def cols(c):
        return pl.ds(pl.multiple_of(c * DC, 128), DC)

    first = lax.rem(rep + 1, R) * CR
    turn = [lax.rem(first + i, C) for i in range(C)]

    for c in range(C):
        local["t", c] = keep(tok_ref.at[:, cols(c)], tokb.at[c, oa], c)
    local["g"] = keep(wg_ref, wgb.at[rep], 2 * C)
    local["u"] = keep(wu_ref, wub.at[rep], 2 * C + 1)
    local["d"] = keep(wd_ref, wdb.at[rep], 2 * C + 2)
    for i in range(C):
        local["c", i] = keep(cot_ref.at[:, cols(turn[i])], cotb.at[turn[i], oa], C + i)

    barrier = pltpu.get_barrier_semaphore()
    for peer in peers:
        pl.semaphore_signal(barrier, inc=1, device_id=peer, device_id_type=MESH)
    pl.semaphore_wait(barrier, len(peers))

    relay = A > 2
    zc = {}
    fc = {}
    later = []

    def sends_itself(j):
        if relay and j == A - 1:
            return oa != 0
        if relay and j == 1:
            return oa != A - 1
        return None

    def guarded(condition, action):
        if condition is None:
            action()
        else:
            pl.when(condition)(action)

    def spread(k, c, src, buf):
        for j in range(1, A):
            copy = build(src.at[:, cols(c)], buf.at[c, oa], zs.at[k, j], zr.at[k, j], out_peer(j))
            zc[k, j] = copy
            guarded(sends_itself(j), copy.start)
            later.append((sends_itself(j), copy))

    def pass_on(k, c, buf):
        if not relay:
            return
        for n, (at, source, j, last, slot) in enumerate(
            ((A - 2, 0, A - 2, A - 1, A - 1), (1, A - 1, 2, 0, 1))
        ):
            copy = build(
                buf.at[c, source], buf.at[c, source], fs.at[k, n], zr.at[k, slot],
                {"ep": last * B + ob},
            )

            def act(copy=copy, j=j):
                zc[k, j].wait_recv()
                copy.start()

            pl.when(oa == at)(act)
            later.append((oa == at, copy))

    def arrive(k):
        for j in range(1, A):
            condition = None
            if relay and j == A - 2:
                condition = oa != A - 2
            if relay and j == 2:
                other = oa != 1
                condition = other if condition is None else jnp.logical_and(condition, other)
            guarded(condition, zc[k, j].wait_recv)

    mc = {}
    for j in range(1, A):
        mc[j] = remote(meta_ref, metab.at[oa], zs.at[2 * C, j], zr.at[2 * C, j], out_peer(j))
    for c in range(C):
        spread(c, c, tok_ref, tokb)
    wc = {}
    for n, (src, dst) in enumerate(((wg_ref, wgb), (wu_ref, wub), (wd_ref, wdb))):
        for j in range(1, R):
            wc[n, j] = remote(src, dst.at[rep], ws.at[n, j], wr.at[n, j], rep_peer(j))
    started += list(mc.values()) + list(wc.values())

    metab[oa] = meta_ref[...]
    BP = slotb.shape[0]
    row = lax.broadcasted_iota(jnp.int32, (BP, T), 0)
    named = jnp.where(row < B, oa * B + lax.rem(ob + row, B), -1).astype(F32)
    earlier = (
        lax.broadcasted_iota(jnp.int32, (T, T), 0) < lax.broadcasted_iota(jnp.int32, (T, T), 1)
    ).astype(F32).astype(BF16)
    for j in range(1, A):
        mc[j].wait_recv()
    for a in range(A):
        member = jnp.zeros((BP, T), F32)
        weight = jnp.zeros((BP, T), F32)
        for k in range(K):
            same = metab[a, k : k + 1, :] == named
            member = member + jnp.where(same, 1.0, 0.0)
            weight = weight + jnp.where(same, metab[a, KP + k : KP + k + 1, :], 0.0)
        place = jnp.dot(member.astype(BF16), earlier, preferred_element_type=F32)
        slotb[:, a * T : (a + 1) * T] = jnp.where(member > 0.5, place + float(a * cap), -1.0)
        gateb[:, a * T : (a + 1) * T] = weight
    starts = [a * cap // 16 * 16 for a in range(A)]
    slot_id = lax.broadcasted_iota(jnp.int32, (S, A * T), 0).astype(F32)
    for b in range(B):
        hit = slotb[b : b + 1, :] == slot_id
        pick[b] = jnp.where(hit, 1.0, 0.0).astype(BF16)
        mix = jnp.where(hit, gateb[b : b + 1, :], 0.0)
        scale[b] = jnp.sum(mix, axis=1, keepdims=True)
        for a in range(A):
            part = mix[starts[a] : starts[a] + W, a * T : (a + 1) * T]
            high = part.astype(BF16)
            mixhi[a, b] = high
            mixlo[a, b] = (part - high.astype(F32)).astype(BF16)

    pc = {}

    def pack_rows(c):
        local["t", c].wait()
        pass_on(c, c, tokb)
        arrive(c)
        source = tokb[c].reshape(A * T, DC)
        packed = jnp.dot(pick[...].reshape(B * S, A * T), source, preferred_element_type=F32)
        for j in list(range(1, B)) + [0]:
            block = packed[j * S : (j + 1) * S].astype(BF16)
            if j == 0:
                recvx[c, 0] = block
            else:
                sendx[c, j] = block
                pc["x", c, j] = remote(
                    sendx.at[c, j], recvx.at[c, j], ps.at[c, j], pr.at[c, j], in_peer(j)
                )

    def pack_grads(i):
        c = turn[i]
        local["c", i].wait()
        arrive(C + i)
        source = cotb[c].reshape(A * T, DC)
        packed = jnp.dot(pick[...].reshape(B * S, A * T), source, preferred_element_type=F32)
        for j in list(range(1, B)) + [0]:
            block = (packed[j * S : (j + 1) * S] * scale[j]).astype(BF16)
            if j == 0:
                recvg[c, 0] = block
            else:
                sendg[c, j] = block
                pc["g", i, j] = remote(
                    sendg.at[c, j], recvg.at[c, j], ps.at[C + i, j], pr.at[C + i, j], in_peer(j)
                )

    for c in range(C):
        pack_rows(c)
        spread(C + c, turn[c], cot_ref, cotb)

    local["g"].wait()
    local["u"].wait()
    for j in range(1, R):
        wc[0, j].wait_recv()
        wc[1, j].wait_recv()
    for c in range(C):
        part = pl.ds((c % CR) * DC, DC)
        for j in range(1, B):
            pc["x", c, j].wait_recv()

        rows = recvx[c].reshape(B * S, DC)
        gate = contract_columns(rows, wgb[c // CR, :, part])
        up = contract_columns(rows, wub[c // CR, :, part])
        if c > 0:
            gate = gate + gacc[...]
            up = up + uacc[...]
        if c < C - 1:
            gacc[...] = gate
            uacc[...] = up
        else:
            silu = gate / (1.0 + jnp.exp(-gate))
            gacc[...] = silu
            hid[...] = (silu * up).astype(BF16)

    local["d"].wait()
    for j in range(1, R):
        wc[2, j].wait_recv()
    for c in range(C):
        part = pl.ds((c % CR) * DC, DC)
        result = jnp.dot(hid[...], wdb[c // CR, :, part], preferred_element_type=F32)
        for j in list(range(1, B)) + [0]:
            block = result[j * S : (j + 1) * S].astype(BF16)
            if j == 0:
                recvo[c, 0] = block
            else:
                sendo[c, j] = block
                pc["o", c, j] = remote(
                    sendo.at[c, j], recvo.at[c, j],
                    ps.at[2 * C + c, j], pr.at[2 * C + c, j], in_peer(-j),
                )
        pass_on(C + c, turn[c], cotb)

    for i in range(C):
        pack_grads(i)

    yc = {}

    def combine(c):
        for j in range(1, B):
            pc["o", c, j].wait_recv()
        for a in range(A):
            rows = recvo[c, :, pl.ds(starts[a], W), :].reshape(B * W, DC)
            total = contract_rows(mixhi[a].reshape(B * W, T), rows)
            total = total + contract_rows(mixlo[a].reshape(B * W, T), rows)
            comb[a] = total
            sendz[c, a] = total.astype(BF16)
        macc[c] = comb[oa]
        for j in range(1, A):
            yc[c, j] = remote(
                sendz.at[c, lax.rem(oa + j, A)], recvz.at[c, j],
                ys.at[c, j], yr.at[c, j], out_peer(j),
            )

    for c in range(C):
        combine(c)

    def shard(ref, index):
        return jnp.concatenate(
            [ref[index * CR + i].reshape(B * S, DC) for i in range(CR)], axis=1
        )

    gc = {}
    for i in range(C):
        part = pl.ds((i % CR) * DC, DC)
        group = i // CR
        for j in range(1, B):
            pc["g", i, j].wait_recv()
        rows = recvg[turn[i]].reshape(B * S, DC)
        value = contract_columns(rows, wdb[lax.rem(rep + 1 + group, R), :, part])
        if i > 0:
            value = value + uacc[...]
        if i < C - 1:
            uacc[...] = value
        else:
            upg[...] = (value * gacc[...]).astype(BF16)
        if i == C - 1:
            for j in range(1, R):
                peer = lax.rem(rep + j, R)
                supb[j] = contract_rows(upg[...], shard(recvx, peer)).astype(BF16)
                gc[0, j] = remote(supb.at[j], rupb.at[j], gs.at[0, j], gr.at[0, j], rep_peer(j))
        block = contract_rows(hid[...], rows).astype(BF16)
        if group < R - 1:
            j = group + 1
            sdnb[j, :, part] = block
            if i % CR == CR - 1:
                gc[1, j] = remote(sdnb.at[j], rdnb.at[j], gs.at[1, j], gr.at[1, j], rep_peer(j))
        else:
            gdn_ref[:, part] = block.astype(F32)

    gup_ref[...] = contract_rows(upg[...], shard(recvx, rep)).astype(BF16).astype(F32)
    for j in range(1, R):
        gc[0, j].wait_recv()
        gup_ref[...] += rupb[j].astype(F32)
        gc[1, j].wait_recv()
        gdn_ref[...] += rdnb[j].astype(F32)

    for c in range(C):
        total = macc[c]
        for j in range(1, A):
            yc[c, j].wait_recv()
            total = total + recvz[c, j].astype(F32)
        mixed_ref[:, c * DC : (c + 1) * DC] = total.astype(BF16)

    started += list(pc.values()) + list(gc.values()) + list(yc.values())
    for copy in started:
        copy.wait_send()
    for condition, copy in later:
        guarded(condition, copy.wait_send)


def local(tokens, expert_ids, gate_weights, cotangent, w_gate, w_up, w_down):
    ep_count, R = lax.axis_size("ep"), lax.axis_size("rep")
    T, D = tokens.shape
    K = expert_ids.shape[1]
    H = w_gate.shape[2]
    cap = T * K // ep_count + 1
    A = outer_of(ep_count)
    B = ep_count // A
    W = max(rows_of((a + 1) * cap, 16) - a * cap // 16 * 16 for a in range(A))
    S = max(a * cap // 16 * 16 for a in range(A)) + W
    DR = D // R
    DC = DR // 2 if DR % 256 == 0 else DR
    C = D // DC
    KP = rows_of(K, 8)
    BP = rows_of(B, 16)
    meta = jnp.concatenate(
        [
            jnp.pad(expert_ids.T.astype(F32), ((0, KP - K), (0, 0)), constant_values=-2.0),
            jnp.pad(gate_weights.T, ((0, KP - K), (0, 0))),
        ]
    )
    dims = (A, B, R, C, T, K, KP, cap, S, D, DC, H, W)
    vmem, dma = pltpu.VMEM, pltpu.SemaphoreType.DMA
    anywhere = pl.BlockSpec(memory_space=pl.ANY)
    inside = pl.BlockSpec(memory_space=pltpu.VMEM)
    blocks = vmem((C, B, S, DC), BF16)
    mixed, gup, gdn = pl.pallas_call(
        functools.partial(kernel, dims),
        out_shape=(
            jax.ShapeDtypeStruct((T, D), BF16),
            jax.ShapeDtypeStruct((H, DR), F32),
            jax.ShapeDtypeStruct((H, DR), F32),
        ),
        in_specs=[inside] + [anywhere] * 5,
        out_specs=[inside] * 3,
        scratch_shapes=[
            vmem((A, 2 * KP, T), F32),
            vmem((C, A, T, DC), BF16),
            vmem((C, A, T, DC), BF16),
            vmem((R, H, DR), BF16),
            vmem((R, H, DR), BF16),
            vmem((R, H, DR), BF16),
            vmem((BP, A * T), F32),
            vmem((BP, A * T), F32),
            vmem((B, S, A * T), BF16),
            vmem((B, S, 1), F32),
            vmem((A, B, W, T), BF16),
            vmem((A, B, W, T), BF16),
            blocks, blocks, blocks, blocks, blocks, blocks,
            vmem((B * S, H), F32),
            vmem((B * S, H), F32),
            vmem((B * S, H), BF16),
            vmem((B * S, H), BF16),
            vmem((A, T, DC), F32),
            vmem((C, T, DC), F32),
            vmem((C, A, T, DC), BF16),
            vmem((C, A, T, DC), BF16),
            vmem((R, H, DR), BF16),
            vmem((R, H, DR), BF16),
            vmem((R, H, DR), BF16),
            vmem((R, H, DR), BF16),
            dma((2 * C + 3,)),
            dma((2 * C + 1, A)), dma((2 * C + 1, A)),
            dma((2 * C, 2)),
            dma((3 * C, B)), dma((3 * C, B)),
            dma((C, A)), dma((C, A)),
            dma((3, R)), dma((3, R)),
            dma((2, R)), dma((2, R)),
        ],
        compiler_params=pltpu.CompilerParams(
            collective_id=0, has_side_effects=True, vmem_limit_bytes=62 * 1024 * 1024
        ),
    )(meta, tokens, cotangent, w_gate[0].T, w_up[0].T, w_down[0])
    return mixed, gup.T[None], gdn[None]


def solution(mesh):
    in_specs = (
        P(("ep", "rep"), None),
        P(("ep", "rep"), None),
        P(("ep", "rep"), None),
        P(("ep", "rep"), None),
        P("ep", "rep", None),
        P("ep", "rep", None),
        P("ep", None, "rep"),
    )
    out_specs = (P(("ep", "rep"), None), P("ep", "rep", None), P("ep", None, "rep"))
    return jax.shard_map(local, mesh=mesh, in_specs=in_specs, out_specs=out_specs, check_vma=False)
```

```python
import functools

import jax
import jax.numpy as jnp
from jax import lax
from jax.experimental import pallas as pl
from jax.experimental.pallas import tpu as pltpu
from jax.sharding import PartitionSpec as P

MESH = pl.DeviceIdType.MESH
F32 = jnp.float32
BF16 = jnp.bfloat16
VMEM_MIB = 60


def rows_of(count, unit):
    return -(-count // unit) * unit


def outer_of(ep_count):
    outer = 1
    while outer * outer < ep_count and ep_count % (outer * 2) == 0:
        outer *= 2
    return outer


def contract_columns(lhs, rhs):
    return lax.dot_general(lhs, rhs, (((1,), (1,)), ((), ())), preferred_element_type=F32)


def contract_rows(lhs, rhs):
    return lax.dot_general(lhs, rhs, (((0,), (0,)), ((), ())), preferred_element_type=F32)


def kernel(
    dims,
    ids_ref, weight_ref, tok_ref, cot_ref, wg_ref, wu_ref, wd_ref,
    mixed_ref, gup_ref, gdn_ref,
    idb, weightb, tokb, cotb, wgb, wub, wdb,
    slotb, gateb, pick, scale, mixhi, mixlo,
    sendx, recvx, sendg, recvg, sendo, recvo,
    gacc, uacc, hid, upg,
    comb, macc, sendz, recvz, supb, rupb, sdnb, rdnb,
    lsem, zs, zr, fs, ps, pr, ys, yr, ws, wr, gs, gr,
):
    A, B, R, C, T, K, cap, S, D, DC, H, W = dims
    CR = C // R
    ep = lax.axis_index("ep")
    rep = lax.axis_index("rep")
    oa, ob = ep // B, ep % B

    def out_peer(j):
        return {"ep": lax.rem(oa + j, A) * B + ob}

    def in_peer(j):
        return {"ep": oa * B + lax.rem(ob + j + B, B)}

    def rep_peer(j):
        return {"rep": lax.rem(rep + j, R)}

    peers = (
        [out_peer(j) for j in range(1, A)]
        + [in_peer(j) for j in range(1, B)]
        + [rep_peer(j) for j in range(1, R)]
    )

    def build(src, dst, ssem, rsem, peer):
        return pltpu.make_async_remote_copy(
            src_ref=src, dst_ref=dst, send_sem=ssem, recv_sem=rsem,
            device_id=peer, device_id_type=MESH,
        )

    def remote(src, dst, ssem, rsem, peer):
        copy = build(src, dst, ssem, rsem, peer)
        copy.start()
        return copy

    started = []
    local = {}

    def keep(src, dst, index):
        copy = pltpu.make_async_copy(src, dst, lsem.at[index])
        copy.start()
        return copy

    def cols(c):
        return pl.ds(pl.multiple_of(c * DC, 128), DC)

    first = lax.rem(rep + 1, R) * CR
    turn = [lax.rem(first + i, C) for i in range(C)]

    for c in range(C):
        local["t", c] = keep(tok_ref.at[:, cols(c)], tokb.at[c, oa], c)
    local["g"] = keep(wg_ref, wgb.at[rep], 2 * C)
    local["u"] = keep(wu_ref, wub.at[rep], 2 * C + 1)
    local["d"] = keep(wd_ref, wdb.at[rep], 2 * C + 2)
    for i in range(C):
        local["c", i] = keep(cot_ref.at[:, cols(turn[i])], cotb.at[turn[i], oa], C + i)

    barrier = pltpu.get_barrier_semaphore()
    for peer in peers:
        pl.semaphore_signal(barrier, inc=1, device_id=peer, device_id_type=MESH)
    pl.semaphore_wait(barrier, len(peers))

    relay = A > 2
    zc = {}
    fc = {}
    later = []

    def sends_itself(j):
        if relay and j == A - 1:
            return oa != 0
        if relay and j == 1:
            return oa != A - 1
        return None

    def guarded(condition, action):
        if condition is None:
            action()
        else:
            pl.when(condition)(action)

    def spread(k, c, src, buf):
        for j in range(1, A):
            copy = build(src.at[:, cols(c)], buf.at[c, oa], zs.at[k, j], zr.at[k, j], out_peer(j))
            zc[k, j] = copy
            guarded(sends_itself(j), copy.start)
            later.append((sends_itself(j), copy))

    def pass_on(k, c, buf):
        if not relay:
            return
        for n, (at, source, j, last, slot) in enumerate(
            ((A - 2, 0, A - 2, A - 1, A - 1), (1, A - 1, 2, 0, 1))
        ):
            copy = build(
                buf.at[c, source], buf.at[c, source], fs.at[k, n], zr.at[k, slot],
                {"ep": last * B + ob},
            )

            def act(copy=copy, j=j):
                zc[k, j].wait_recv()
                copy.start()

            pl.when(oa == at)(act)
            later.append((oa == at, copy))

    def arrive(k):
        for j in range(1, A):
            condition = None
            if relay and j == A - 2:
                condition = oa != A - 2
            if relay and j == 2:
                other = oa != 1
                condition = other if condition is None else jnp.logical_and(condition, other)
            guarded(condition, zc[k, j].wait_recv)

    mc = {}
    for j in range(1, A):
        for n, (src, dst) in enumerate(((ids_ref, idb), (weight_ref, weightb))):
            mc[n, j] = remote(
                src, dst.at[oa], zs.at[2 * C + n, j], zr.at[2 * C + n, j], out_peer(j)
            )
    for c in range(C):
        spread(c, c, tok_ref, tokb)
    wc = {}
    for n, (src, dst) in enumerate(((wg_ref, wgb), (wu_ref, wub), (wd_ref, wdb))):
        for j in range(1, R):
            wc[n, j] = remote(src, dst.at[rep], ws.at[n, j], wr.at[n, j], rep_peer(j))
    started += list(mc.values()) + list(wc.values())

    idb[oa] = ids_ref[...]
    weightb[oa] = weight_ref[...]
    BP = slotb.shape[0]
    row = lax.broadcasted_iota(jnp.int32, (BP, T), 0)
    named = jnp.where(row < B, oa * B + lax.rem(ob + row, B), -1)
    earlier = (
        lax.broadcasted_iota(jnp.int32, (T, T), 0) < lax.broadcasted_iota(jnp.int32, (T, T), 1)
    ).astype(F32).astype(BF16)
    for j in range(1, A):
        mc[0, j].wait_recv()
        mc[1, j].wait_recv()
    for a in range(A):
        member = jnp.zeros((BP, T), F32)
        weight = jnp.zeros((BP, T), F32)
        for k in range(K):
            same = idb[a, k : k + 1, :] == named
            member = member + jnp.where(same, 1.0, 0.0)
            weight = weight + jnp.where(same, weightb[a, k : k + 1, :], 0.0)
        place = jnp.dot(member.astype(BF16), earlier, preferred_element_type=F32)
        slotb[:, a * T : (a + 1) * T] = jnp.where(member > 0.5, place + float(a * cap), -1.0)
        gateb[:, a * T : (a + 1) * T] = weight
    starts = [a * cap // 16 * 16 for a in range(A)]
    slot_id = lax.broadcasted_iota(jnp.int32, (S, A * T), 0).astype(F32)
    for b in range(B):
        hit = slotb[b : b + 1, :] == slot_id
        pick[b] = jnp.where(hit, 1.0, 0.0).astype(BF16)
        mix = jnp.where(hit, gateb[b : b + 1, :], 0.0)
        scale[b] = jnp.sum(mix, axis=1, keepdims=True)
        for a in range(A):
            part = mix[starts[a] : starts[a] + W, a * T : (a + 1) * T]
            high = part.astype(BF16)
            mixhi[a, b] = high
            mixlo[a, b] = (part - high.astype(F32)).astype(BF16)

    pc = {}

    def pack_rows(c):
        local["t", c].wait()
        pass_on(c, c, tokb)
        arrive(c)
        source = tokb[c].reshape(A * T, DC)
        packed = jnp.dot(pick[...].reshape(B * S, A * T), source, preferred_element_type=F32)
        for j in list(range(1, B)) + [0]:
            block = packed[j * S : (j + 1) * S].astype(BF16)
            if j == 0:
                recvx[c, 0] = block
            else:
                sendx[c, j] = block
                pc["x", c, j] = remote(
                    sendx.at[c, j], recvx.at[c, j], ps.at[c, j], pr.at[c, j], in_peer(j)
                )

    def pack_grads(i):
        c = turn[i]
        local["c", i].wait()
        arrive(C + i)
        source = cotb[c].reshape(A * T, DC)
        packed = jnp.dot(pick[...].reshape(B * S, A * T), source, preferred_element_type=F32)
        for j in list(range(1, B)) + [0]:
            block = (packed[j * S : (j + 1) * S] * scale[j]).astype(BF16)
            if j == 0:
                recvg[c, 0] = block
            else:
                sendg[c, j] = block
                pc["g", i, j] = remote(
                    sendg.at[c, j], recvg.at[c, j], ps.at[C + i, j], pr.at[C + i, j], in_peer(j)
                )

    for c in range(C):
        pack_rows(c)
        spread(C + c, turn[c], cot_ref, cotb)

    local["g"].wait()
    local["u"].wait()
    for j in range(1, R):
        wc[0, j].wait_recv()
        wc[1, j].wait_recv()
    for c in range(C):
        part = pl.ds((c % CR) * DC, DC)
        if c == C - 1:
            pass_on(C, turn[0], cotb)
            pack_grads(0)
        for j in range(1, B):
            pc["x", c, j].wait_recv()

        rows = recvx[c].reshape(B * S, DC)
        gate = contract_columns(rows, wgb[c // CR, :, part])
        up = contract_columns(rows, wub[c // CR, :, part])
        if c > 0:
            gate = gate + gacc[...]
            up = up + uacc[...]
        if c < C - 1:
            gacc[...] = gate
            uacc[...] = up
        else:
            silu = gate / (1.0 + jnp.exp(-gate))
            gacc[...] = silu
            hid[...] = (silu * up).astype(BF16)

    local["d"].wait()
    for j in range(1, R):
        wc[2, j].wait_recv()
    for c in range(C):
        part = pl.ds((c % CR) * DC, DC)
        result = jnp.dot(hid[...], wdb[c // CR, :, part], preferred_element_type=F32)
        for j in list(range(1, B)) + [0]:
            block = result[j * S : (j + 1) * S].astype(BF16)
            if j == 0:
                recvo[c, 0] = block
            else:
                sendo[c, j] = block
                pc["o", c, j] = remote(
                    sendo.at[c, j], recvo.at[c, j],
                    ps.at[2 * C + c, j], pr.at[2 * C + c, j], in_peer(-j),
                )
        if c > 0:
            pass_on(C + c, turn[c], cotb)

    for i in range(1, C):
        pack_grads(i)

    yc = {}

    def combine(c):
        for j in range(1, B):
            pc["o", c, j].wait_recv()
        for a in range(A):
            rows = recvo[c, :, pl.ds(starts[a], W), :].reshape(B * W, DC)
            total = contract_rows(mixhi[a].reshape(B * W, T), rows)
            total = total + contract_rows(mixlo[a].reshape(B * W, T), rows)
            comb[a] = total
            sendz[c, a] = total.astype(BF16)
        macc[c] = comb[oa]
        for j in range(1, A):
            yc[c, j] = remote(
                sendz.at[c, lax.rem(oa + j, A)], recvz.at[c, j],
                ys.at[c, j], yr.at[c, j], out_peer(j),
            )

    def shard(ref, index):
        return jnp.concatenate(
            [ref[index * CR + i].reshape(B * S, DC) for i in range(CR)], axis=1
        )

    gc = {}

    def back(i):
        part = pl.ds((i % CR) * DC, DC)
        group = i // CR
        for j in range(1, B):
            pc["g", i, j].wait_recv()
        rows = recvg[turn[i]].reshape(B * S, DC)
        value = contract_columns(rows, wdb[lax.rem(rep + 1 + group, R), :, part])
        if i > 0:
            value = value + uacc[...]
        if i < C - 1:
            uacc[...] = value
        else:
            upg[...] = (value * gacc[...]).astype(BF16)
        if i == C - 1:
            for j in range(1, R):
                peer = lax.rem(rep + j, R)
                supb[j] = contract_rows(upg[...], shard(recvx, peer)).astype(BF16)
                gc[0, j] = remote(supb.at[j], rupb.at[j], gs.at[0, j], gr.at[0, j], rep_peer(j))
        block = contract_rows(hid[...], rows).astype(BF16)
        if group < R - 1:
            j = group + 1
            sdnb[j, :, part] = block
            if i % CR == CR - 1:
                gc[1, j] = remote(sdnb.at[j], rdnb.at[j], gs.at[1, j], gr.at[1, j], rep_peer(j))
        else:
            gdn_ref[:, part] = block.astype(F32)

    back(0)
    for c in range(C):
        combine(c)
        if c > 0:
            back(c)

    gup_ref[...] = contract_rows(upg[...], shard(recvx, rep)).astype(BF16).astype(F32)
    for j in range(1, R):
        gc[0, j].wait_recv()
        gup_ref[...] += rupb[j].astype(F32)
        gc[1, j].wait_recv()
        gdn_ref[...] += rdnb[j].astype(F32)

    for c in range(C):
        total = macc[c]
        for j in range(1, A):
            yc[c, j].wait_recv()
            total = total + recvz[c, j].astype(F32)
        mixed_ref[:, c * DC : (c + 1) * DC] = total.astype(BF16)

    started += list(pc.values()) + list(gc.values()) + list(yc.values())
    for copy in started:
        copy.wait_send()
    for condition, copy in later:
        guarded(condition, copy.wait_send)


def local(tokens, expert_ids, gate_weights, cotangent, w_gate, w_up, w_down):
    ep_count, R = lax.axis_size("ep"), lax.axis_size("rep")
    T, D = tokens.shape
    K = expert_ids.shape[1]
    H = w_gate.shape[2]
    cap = T * K // ep_count + 1
    A = outer_of(ep_count)
    B = ep_count // A
    W = max(rows_of((a + 1) * cap, 16) - a * cap // 16 * 16 for a in range(A))
    S = max(a * cap // 16 * 16 for a in range(A)) + W
    DR = D // R
    DC = DR // 2 if DR % 256 == 0 else DR
    C = D // DC
    BP = rows_of(B, 16)
    dims = (A, B, R, C, T, K, cap, S, D, DC, H, W)
    vmem, dma = pltpu.VMEM, pltpu.SemaphoreType.DMA
    anywhere = pl.BlockSpec(memory_space=pl.ANY)
    inside = pl.BlockSpec(memory_space=pltpu.VMEM)
    blocks = vmem((C, B, S, DC), BF16)
    mixed, gup, gdn = pl.pallas_call(
        functools.partial(kernel, dims),
        out_shape=(
            jax.ShapeDtypeStruct((T, D), BF16),
            jax.ShapeDtypeStruct((H, DR), F32),
            jax.ShapeDtypeStruct((H, DR), F32),
        ),
        in_specs=[inside] * 2 + [anywhere] * 5,
        out_specs=[inside] * 3,
        scratch_shapes=[
            vmem((A, K, T), jnp.int32),
            vmem((A, K, T), F32),
            vmem((C, A, T, DC), BF16),
            vmem((C, A, T, DC), BF16),
            vmem((R, H, DR), BF16),
            vmem((R, H, DR), BF16),
            vmem((R, H, DR), BF16),
            vmem((BP, A * T), F32),
            vmem((BP, A * T), F32),
            vmem((B, S, A * T), BF16),
            vmem((B, S, 1), F32),
            vmem((A, B, W, T), BF16),
            vmem((A, B, W, T), BF16),
            blocks, blocks, blocks, blocks, blocks, blocks,
            vmem((B * S, H), F32),
            vmem((B * S, H), F32),
            vmem((B * S, H), BF16),
            vmem((B * S, H), BF16),
            vmem((A, T, DC), F32),
            vmem((C, T, DC), F32),
            vmem((C, A, T, DC), BF16),
            vmem((C, A, T, DC), BF16),
            vmem((R, H, DR), BF16),
            vmem((R, H, DR), BF16),
            vmem((R, H, DR), BF16),
            vmem((R, H, DR), BF16),
            dma((2 * C + 3,)),
            dma((2 * C + 2, A)), dma((2 * C + 2, A)),
            dma((2 * C, 2)),
            dma((3 * C, B)), dma((3 * C, B)),
            dma((C, A)), dma((C, A)),
            dma((3, R)), dma((3, R)),
            dma((2, R)), dma((2, R)),
        ],
        compiler_params=pltpu.CompilerParams(
            collective_id=0, has_side_effects=True, vmem_limit_bytes=VMEM_MIB * 1024 * 1024
        ),
    )(expert_ids.T, gate_weights.T, tokens, cotangent, w_gate[0].T, w_up[0].T, w_down[0])
    return mixed, gup.T[None], gdn[None]


def solution(mesh):
    in_specs = (
        P(("ep", "rep"), None),
        P(("ep", "rep"), None),
        P(("ep", "rep"), None),
        P(("ep", "rep"), None),
        P("ep", "rep", None),
        P("ep", "rep", None),
        P("ep", None, "rep"),
    )
    out_specs = (P(("ep", "rep"), None), P("ep", "rep", None), P("ep", None, "rep"))
    return jax.shard_map(local, mesh=mesh, in_specs=in_specs, out_specs=out_specs, check_vma=False)
```
